512 devices in a mesh: expert: 64 (over y, x, core), hidden: 8 (over z).
Axes of the slice: x: 4, y: 8, z: 8, core: 2. Of those that a mesh axis runs over, the one named last changes fastest.
Arguments:
- tokens: bfloat16 [4096, 4096], P('expert', 'hidden'), may hold values from -6 to 6
- expert_ids: int32 [4096, 8], P('expert'), may hold values from 0 to 63, all different within a row; in each aligned block of 64 rows (0 to 63, 64 to 127, ...) at most 16 rows name the same one
- gate_weights: float32 [4096, 8], P('expert'), may hold values from 0.05 to 0.5
- gate_proj: bfloat16 [64, 1536, 4096], P('expert', 'hidden'), may hold values from -0.09375 to 0.09375
- up_proj: bfloat16 [64, 1536, 4096], P('expert', 'hidden'), may hold values from -0.09375 to 0.09375
- down_proj: bfloat16 [64, 1536, 4096], P('expert', None, 'hidden'), may hold values from -0.15625 to 0.15625
Outputs:
- moe_out: bfloat16 [4096, 4096], P('expert', 'hidden')
The draws below stay inside these ranges and needn't reach their ends.
Inputs may be any that keep to these rules, and one draw needn't show every extreme that they name: `expert_ids`: each row names 8 different experts; in each aligned block of 64 rows no expert is named by more than 16 rows.
All inputs are finite; a program needn't handle non-finite values.
Results may differ from the reference program's by a relative error of at most 0.0057.
Values may be sent and summed in bfloat16 or wider, within the bound.
No kernel may reach another device: no remote copies, remote signals or barrier semaphores. Data moves between devices by JAX's collectives and lax.ppermute only.
A program may use at most 64 MiB of HBM per device.

```python
import math
import jax
import jax.numpy as jnp
import numpy as np
from jax import lax

D = 4096
FF = 1536
TOP = 8
TOK_DEV = 64
EXPERTS = 64
TOKENS = 4096
CAP = 16
N_EXPERT = 64


def block_scale(rng, extent, shards, low, high):
    gain, own = 1.0, jax.random.fold_in(rng, 6)
    for dim, parts in shards:
        draws = jnp.exp(jax.random.uniform(jax.random.fold_in(own, dim), (parts,), jnp.float32, low / len(shards), high / len(shards)))
        gain = gain * jnp.repeat(draws, extent[dim] // parts).reshape([-1 if axis == dim else 1 for axis in range(len(extent))])
    return gain


def deal_out(key, own, number, rows, count, top, bound, lean):
    ranking = jax.random.permutation(key, count)
    heavy_load, ordinary = portions_of(count, rows * top, bound, lean, True), portions_of(count, rows * top, bound, lean, False)
    places = jnp.arange(count)

    def named(sizes, rotation):
        used = int((sizes > 0).sum())
        fixed = max(1, used // 4)
        passed = fixed + (places - fixed + rotation * (used - fixed)) % max(1, count - fixed)
        return jnp.zeros((count,), jnp.int32).at[ranking[jnp.where(places < fixed, places, passed)]].set(jnp.asarray(sizes, jnp.int32))

    sizes = jnp.where(number % 4 == 0, named(heavy_load, number // 4), named(ordinary, number - number // 4 - 1))
    mixed = jax.random.permutation(jax.random.fold_in(own, 3), count)
    giver, sink = mixed[0:count // 2 * 2:2], mixed[1:count // 2 * 2:2]
    margin = jnp.minimum(sizes[giver] - 1, bound - sizes[sink]) // 2
    margin = jnp.where((giver == ranking[0]) | (sink == ranking[0]) | (sizes[sink] == 0), 0, jnp.maximum(margin, 0))
    passed = jax.random.randint(jax.random.fold_in(own, 4), (count // 2,), 0, 1 << 20) % (margin + 1)
    sizes = sizes.at[giver].add(-passed).at[sink].add(passed)
    labels = jnp.searchsorted(jnp.cumsum(sizes), jnp.arange(rows * top), side="right").astype(jnp.int32)
    listing = labels.reshape(top, rows).T
    listing = listing[jax.random.permutation(jax.random.fold_in(own, 1), rows)]
    rotation = jax.random.randint(jax.random.fold_in(own, 2), (rows, 1), 0, top)
    return jnp.take_along_axis(listing, (jnp.arange(top)[None, :] + rotation) % top, axis=1)


def portions_of(count, total, most, slope, full):
    weights = [(1 << 20) // math.isqrt(standing ** slope) + 1 for standing in range(1, count + 1)]
    largest = most if full else min(most, max(-(-total // count), total * weights[0] // sum(weights)))
    least = 1 if total - largest >= count - 1 else 0
    given, surplus = [largest] + [least] * (count - 1), total - largest - least * (count - 1)
    while surplus > 0:
        free = [i for i in range(1, count) if given[i] < largest] or [i for i in range(1, count) if given[i] < most]
        pool, remaining = sum([weights[i] for i in free]), surplus
        for i in free:
            addition = min(most - given[i], max(1, remaining * weights[i] // pool), surplus)
            given[i] = given[i] + addition
            surplus = surplus - addition
    return np.array(given)


def centred(rng, dims, scale, bound, pieces=(), held_as=jnp.bfloat16):
    drawn = jax.random.normal(rng, dims, jnp.float32) * scale
    if len(pieces) > 0:
        drawn = block_scale(rng, dims, pieces, -0.22, 0.18) * drawn
    return jnp.clip(drawn, min=-bound, max=bound).astype(held_as)


def setup_inputs(seed: int = 0) -> dict:
    arg_keys = jax.random.split(jax.random.key(seed), 7)
    tokens = centred(arg_keys[0], (TOKENS, D), 1.0, 6.0, ((0, 64), (1, 8)))
    expert_ids_keys = jax.random.split(jax.random.fold_in(arg_keys[1], 1), TOKENS // TOK_DEV)
    expert_ids_turns = jax.random.permutation(jax.random.fold_in(arg_keys[1], 3), TOKENS // TOK_DEV)
    expert_ids = jax.vmap(lambda own, number: deal_out(jax.random.fold_in(arg_keys[1], 2), own, number, TOK_DEV, EXPERTS, TOP, CAP, 2))(expert_ids_keys, expert_ids_turns).reshape((TOKENS, TOP))
    gate_weights = jnp.clip(jnp.exp(math.log(0.5) - 2.3025851 * jax.random.uniform(arg_keys[2], (TOKENS, TOP), jnp.float32) ** block_scale(arg_keys[2], (TOKENS, TOP), ((0, 64),), -0.2, 0.2)), 0.05, 0.5)
    gate_proj = centred(arg_keys[3], (EXPERTS, FF, D), D ** -0.5, 0.09375, ((0, 64), (1, 8)))
    up_proj = centred(arg_keys[4], (EXPERTS, FF, D), D ** -0.5, 0.09375, ((0, 64), (1, 8)))
    down_proj = centred(arg_keys[5], (EXPERTS, FF, D), FF ** -0.5, 0.15625, ((0, 64), (2, 8)))
    return {"tokens": tokens, "expert_ids": expert_ids, "gate_weights": gate_weights, "gate_proj": gate_proj, "up_proj": up_proj, "down_proj": down_proj}


def reference(tokens, expert_ids, gate_weights, gate_proj, up_proj, down_proj):
    flat_ids = expert_ids.reshape(-1).astype(jnp.int32)
    onehot = (flat_ids[:, None] == jnp.arange(EXPERTS, dtype=jnp.int32)[None, :]).astype(jnp.int32)
    blocks = onehot.reshape(N_EXPERT, TOK_DEV * TOP, EXPERTS)
    ranks = jnp.cumsum(blocks, axis=1) - blocks
    slot_index = jnp.sum(ranks * blocks, axis=2).reshape(-1).astype(jnp.int32)
    pair_index = jnp.arange(TOKENS * TOP, dtype=jnp.int32)
    source_block = pair_index // (TOK_DEV * TOP)
    position = (source_block * CAP + slot_index).astype(jnp.int32)
    token_index = (pair_index // TOP).astype(jnp.int32)
    row_token = jnp.zeros((EXPERTS, N_EXPERT * CAP), jnp.int32).at[flat_ids, position].set(token_index)
    row_gate = jnp.zeros((EXPERTS, N_EXPERT * CAP), gate_weights.dtype).at[flat_ids, position].set(gate_weights.reshape(-1))

    def expert_step(running, inputs):
        w_gate, w_up, w_down, rows_idx, rows_gate = inputs
        picked = tokens[rows_idx]
        gate_sum = jnp.dot(picked, w_gate.T, preferred_element_type=jnp.float32)
        up_sum = jnp.dot(picked, w_up.T, preferred_element_type=jnp.float32)
        activation = (jax.nn.silu(gate_sum) * up_sum).astype(jnp.bfloat16)
        expert_out = jnp.dot(activation, w_down, preferred_element_type=jnp.float32).astype(jnp.bfloat16)
        weighted = rows_gate[:, None] * expert_out.astype(jnp.float32)
        return running.at[rows_idx].add(weighted), None

    start_sum = jnp.zeros((TOKENS, D), jnp.float32)
    mixed, _ = lax.scan(expert_step, start_sum, (gate_proj, up_proj, down_proj, row_token, row_gate))
    return mixed.astype(jnp.bfloat16)
```

```python
import functools

import jax
import jax.numpy as jnp
from jax import lax
from jax.experimental import pallas as pl
from jax.experimental.pallas import tpu as pltpu
from jax.sharding import PartitionSpec as P

BF16 = jnp.bfloat16
F32 = jnp.float32


def pack_kernel(ids_ref, tokens_ref, packed_ref, slots_ref):
    experts, tok_rows = slots_ref.shape
    lo, wide = packed_ref.shape[1:]
    width = tokens_ref.shape[1]
    expert = lax.broadcasted_iota(jnp.int32, (experts, tok_rows), 0)
    chosen = expert == ids_ref[0:1, :]
    for k in range(1, ids_ref.shape[0]):
        chosen = jnp.logical_or(chosen, expert == ids_ref[k : k + 1, :])
    before = lax.broadcasted_iota(jnp.int32, (tok_rows, tok_rows), 0)
    after = lax.broadcasted_iota(jnp.int32, (tok_rows, tok_rows), 1)
    earlier = jnp.where(before < after, 1.0, 0.0).astype(BF16)
    ranks = jnp.dot(jnp.where(chosen, 1.0, 0.0).astype(BF16), earlier, preferred_element_type=F32)
    slots = jnp.where(chosen, ranks, -1.0)
    slots_ref[...] = slots
    slot = lax.broadcasted_iota(jnp.int32, (experts, lo, tok_rows), 1).astype(F32)
    spread = jnp.broadcast_to(slots[:, None, :], (experts, lo, tok_rows))
    first = jnp.where(spread == slot, 1.0, 0.0).reshape(experts * lo, tok_rows).astype(BF16)
    rest = jnp.where(spread == slot + lo, 1.0, 0.0).reshape(experts * lo, tok_rows).astype(BF16)
    values = jnp.dot(first, tokens_ref[...], preferred_element_type=F32)
    packed_ref[:, :, :width] = values.reshape(experts, lo, width).astype(BF16)
    values = jnp.dot(rest, tokens_ref[:, : wide - width], preferred_element_type=F32)
    packed_ref[:, :, width:] = values.reshape(experts, lo, wide - width).astype(BF16)


def pack_rows(ids, tokens, experts, lo, near):
    tok_rows, width = tokens.shape
    return pl.pallas_call(
        pack_kernel,
        out_shape=(
            jax.ShapeDtypeStruct((experts, lo, width + near), BF16),
            jax.ShapeDtypeStruct((experts, tok_rows), F32),
        ),
        in_specs=[pl.BlockSpec(memory_space=pltpu.VMEM)] * 2,
        out_specs=[pl.BlockSpec(memory_space=pltpu.VMEM)] * 2,
        name="pack_rows",
    )(ids, tokens)


def hidden_kernel(lo, full_ref, weight_ref, far_ref, act_ref, total_ref):
    step = pl.program_id(0)
    per, rows, wide = full_ref.shape
    width, units = weight_ref.shape[1], weight_ref.shape[2] // 2
    near = wide - width
    first = rest = None
    for i in range(per):
        weight = weight_ref[i]
        more = jnp.dot(full_ref[i, :, :width], weight, preferred_element_type=F32)
        first = more if first is None else first + more
        more = jnp.dot(full_ref[i, :, width:], weight[:near], preferred_element_type=F32)
        rest = more if rest is None else rest + more

    @pl.when(step == 0)
    def _():
        total_ref[0] = first
        total_ref[1] = rest + far_ref[...]

    @pl.when(step > 0)
    def _():
        total_ref[0] += first
        total_ref[1] += rest

    @pl.when(step == pl.num_programs(0) - 1)
    def _():
        halves = [total_ref[group].reshape(rows // lo, lo, 2 * units) for group in range(2)]
        total = jnp.concatenate(halves, axis=1).reshape(2 * rows, 2 * units).T
        gate = total[:units]
        act_ref[...] = (gate / (1.0 + jnp.exp(-gate)) * total[units:]).astype(BF16)


def hidden_units(full, weight, far_sums, lo):
    n_hidden, rows, wide = full.shape
    width, pair = weight.shape[1:]
    per = 4
    return pl.pallas_call(
        functools.partial(hidden_kernel, lo),
        grid=(n_hidden // per,),
        out_shape=jax.ShapeDtypeStruct((pair // 2, rows * 2), BF16),
        in_specs=[
            pl.BlockSpec((per, rows, wide), lambda h: (h, 0, 0)),
            pl.BlockSpec((per, width, pair), lambda h: (h, 0, 0)),
            pl.BlockSpec((rows, pair), lambda h: (0, 0)),
        ],
        out_specs=pl.BlockSpec((pair // 2, rows * 2), lambda h: (0, 0)),
        scratch_shapes=[pltpu.VMEM((2, rows, pair), F32)],
        compiler_params=pltpu.CompilerParams(vmem_limit_bytes=56 << 20),
        name="hidden_units",
    )(full, weight, far_sums)


def on_device(tokens, expert_ids, gate_weights, gate_proj, up_proj, down_proj):
    n_hidden = lax.axis_size("hidden")
    here = lax.axis_index("hidden")
    experts_all = gate_proj.shape[0] * lax.axis_size("expert")
    tok_rows, width = tokens.shape
    top_count = expert_ids.shape[1]
    capacity = 2 * tok_rows * top_count // experts_all
    lo = capacity // 2
    near = width // 2
    rows = experts_all * lo

    def exchange(values):
        return lax.all_to_all(values, "expert", split_axis=0, concat_axis=0, tiled=True)

    packed, slots = pack_rows(expert_ids.T, tokens, experts_all, lo, near)
    packed, far = lax.optimization_barrier((packed, tokens[:, near:]))
    arrived = exchange(packed)
    reach = 1
    while reach < n_hidden:
        other = lax.ppermute(far, "hidden", [(i, i ^ reach) for i in range(n_hidden)])
        upper = (here & reach) != 0
        far = jnp.concatenate([jnp.where(upper, other, far), jnp.where(upper, far, other)], axis=1)
        reach *= 2
    picks = slots[:, None, :] == jnp.arange(capacity, dtype=F32)[None, :, None]
    packed_far = jnp.einsum(
        "est,td->esd", picks[:, lo:].astype(BF16), far, preferred_element_type=F32
    ).astype(BF16)
    arrived, packed_far = lax.optimization_barrier((arrived, packed_far))
    full = lax.all_gather(arrived.reshape(rows, width + near), "hidden", axis=0, tiled=False)
    arrived_far = exchange(packed_far).reshape(rows, n_hidden * (width - near))
    weight = jnp.concatenate([gate_proj[0], up_proj[0]], axis=0).T.reshape(n_hidden, width, -1)
    far_weight = weight[:, near:].reshape(n_hidden * (width - near), -1)
    far_sums = jnp.dot(arrived_far, far_weight, preferred_element_type=F32)
    activation = hidden_units(full, weight, far_sums, lo)
    expert_out = jnp.einsum(
        "fr,fd->rd",
        lax.all_gather(activation, "hidden", axis=0, tiled=True),
        down_proj[0],
        preferred_element_type=F32,
    ).astype(BF16)
    returned = exchange(expert_out.reshape(experts_all, capacity, width))
    hits = expert_ids[:, :, None] == jnp.arange(experts_all, dtype=jnp.int32)
    weights = jnp.sum(jnp.where(hits, gate_weights[:, :, None], 0.0), axis=1)
    combine = jnp.where(picks, weights.T[:, None, :], 0.0)
    mixed = jnp.einsum(
        "est,esd->td",
        combine,
        returned.astype(F32),
        precision=lax.Precision.HIGHEST,
        preferred_element_type=F32,
    )
    return mixed.astype(BF16)


def solution(mesh):
    in_specs = (
        P("expert", "hidden"),
        P("expert", None),
        P("expert", None),
        P("expert", "hidden", None),
        P("expert", "hidden", None),
        P("expert", None, "hidden"),
    )
    out_specs = P("expert", "hidden")
    return jax.shard_map(
        on_device, mesh=mesh, in_specs=in_specs, out_specs=out_specs, check_vma=False
    )
```

```python
import jax
import jax.numpy as jnp
from jax import lax
from jax.experimental import pallas as pl
from jax.experimental.pallas import tpu as pltpu
from jax.sharding import PartitionSpec as P

BF16 = jnp.bfloat16
F32 = jnp.float32


def pack_kernel(ids_ref, tokens_ref, first_ref, rest_ref, slots_ref):
    experts, tok_rows = slots_ref.shape
    lo = first_ref.shape[1]
    width = tokens_ref.shape[1]
    expert = lax.broadcasted_iota(jnp.int32, (experts, tok_rows), 0)
    chosen = expert == ids_ref[0:1, :]
    for k in range(1, ids_ref.shape[0]):
        chosen = jnp.logical_or(chosen, expert == ids_ref[k : k + 1, :])
    before = lax.broadcasted_iota(jnp.int32, (tok_rows, tok_rows), 0)
    after = lax.broadcasted_iota(jnp.int32, (tok_rows, tok_rows), 1)
    earlier = jnp.where(before < after, 1.0, 0.0).astype(BF16)
    ranks = jnp.dot(jnp.where(chosen, 1.0, 0.0).astype(BF16), earlier, preferred_element_type=F32)
    slots = jnp.where(chosen, ranks, -1.0)
    slots_ref[...] = slots
    slot = lax.broadcasted_iota(jnp.int32, (experts, lo, tok_rows), 1).astype(F32)
    spread = jnp.broadcast_to(slots[:, None, :], (experts, lo, tok_rows))
    for group, packed_ref in enumerate((first_ref, rest_ref)):
        picks = jnp.where(spread == slot + lo * group, 1.0, 0.0).reshape(experts * lo, tok_rows).astype(BF16)
        values = jnp.dot(picks, tokens_ref[...], preferred_element_type=F32)
        packed_ref[...] = values.reshape(experts, lo, width).astype(BF16)


def pack_rows(ids, tokens, experts, lo):
    tok_rows, width = tokens.shape
    packed = jax.ShapeDtypeStruct((experts, lo, width), BF16)
    return pl.pallas_call(
        pack_kernel,
        out_shape=(packed, packed, jax.ShapeDtypeStruct((experts, tok_rows), F32)),
        in_specs=[pl.BlockSpec(memory_space=pltpu.VMEM)] * 2,
        out_specs=[pl.BlockSpec(memory_space=pltpu.VMEM)] * 3,
        name="pack_rows",
    )(ids, tokens)


def on_device(tokens, expert_ids, gate_weights, gate_proj, up_proj, down_proj):
    n_hidden = lax.axis_size("hidden")
    here = lax.axis_index("hidden")
    experts_all = gate_proj.shape[0] * lax.axis_size("expert")
    tok_rows, width = tokens.shape
    units = gate_proj.shape[1]
    top_count = expert_ids.shape[1]
    capacity = 2 * tok_rows * top_count // experts_all
    lo = capacity // 2
    rows = experts_all * lo
    across = n_hidden // 2

    def exchange(values):
        return lax.all_to_all(values, "expert", split_axis=0, concat_axis=0, tiled=True)

    def fetch(values, ahead):
        return lax.ppermute(values, "hidden", [(i, (i - ahead) % n_hidden) for i in range(n_hidden)])

    def around(values):
        ahead = behind = values
        yield 0, values
        for step in range(1, across):
            behind, ahead = fetch(behind, -1), fetch(ahead, 1)
            yield n_hidden - step, behind
            yield step, ahead

    first, rest, slots = pack_rows(expert_ids.T, tokens, experts_all, lo)

    both = jnp.concatenate([gate_proj[0], up_proj[0]], axis=0)
    both = lax.dynamic_slice_in_dim(jnp.concatenate([both, both], axis=1), here * width, n_hidden * width, axis=1)
    down = lax.dynamic_slice_in_dim(
        jnp.concatenate([down_proj[0], down_proj[0]], axis=0), here * units, n_hidden * units, axis=0
    )
    first, own = lax.optimization_barrier((first, tokens))
    arrived = exchange(first)
    opposite = fetch(own, across)
    picks = slots[:, None, :] == jnp.arange(capacity, dtype=F32)[None, :, None]
    packed = jnp.concatenate(
        [
            jnp.einsum(
                "est,td->esd", picks[:, group * lo : (group + 1) * lo].astype(BF16), opposite, preferred_element_type=F32
            ).astype(BF16)
            for group in range(2)
        ],
        axis=2,
    )
    arrived, rest, both, down = lax.optimization_barrier((arrived, rest, both, down))
    arrived = [arrived, exchange(rest)]
    arrived[1], packed = lax.optimization_barrier((arrived[1], packed))
    opposite = exchange(packed).reshape(rows, 2 * width)

    activation = []
    for group in range(2):
        total = 0.0
        blocks = list(around(arrived[group].reshape(rows, width)))
        blocks.insert(-2, (across, opposite[:, group * width : (group + 1) * width]))
        for ahead, block in blocks:
            weight = both[:, ahead * width : (ahead + 1) * width]
            total = total + jnp.einsum("fd,rd->fr", weight, block, preferred_element_type=F32)
        activation.append((jax.nn.silu(total[:units]) * total[units:]).astype(BF16))
    activation = jnp.concatenate(activation, axis=1)

    hits = expert_ids[:, :, None] == jnp.arange(experts_all, dtype=jnp.int32)
    weights = jnp.sum(jnp.where(hits, gate_weights[:, :, None], 0.0), axis=1)
    combine = jnp.where(picks, weights.T[:, None, :], 0.0)

    def out_sums(block, ahead):
        return jnp.einsum("fr,fd->rd", block, down[ahead * units : (ahead + 1) * units], preferred_element_type=F32)

    blocks = list(around(activation))
    total = 0.0
    for ahead, block in blocks:
        total = total + out_sums(block, ahead)
    (_, behind), (_, ahead) = blocks[-2:]
    opposite = jnp.concatenate([fetch(behind[:, :rows], -1), fetch(ahead[:, rows:], 1)], axis=1)
    total = (total + out_sums(opposite, across)).astype(BF16)
    total = total.reshape(2, experts_all, lo, width).transpose(1, 0, 2, 3).reshape(experts_all, capacity, width)
    returned = exchange(total)
    mixed = jnp.einsum(
        "est,esd->td",
        combine,
        returned.astype(F32),
        precision=lax.Precision.HIGHEST,
        preferred_element_type=F32,
    )
    return mixed.astype(BF16)


def solution(mesh):
    in_specs = (
        P("expert", "hidden"),
        P("expert", None),
        P("expert", None),
        P("expert", "hidden", None),
        P("expert", "hidden", None),
        P("expert", None, "hidden"),
    )
    out_specs = P("expert", "hidden")
    return jax.shard_map(
        on_device, mesh=mesh, in_specs=in_specs, out_specs=out_specs, check_vma=False
    )
```

```python
import jax
import jax.numpy as jnp
from jax import lax
from jax.experimental import pallas as pl
from jax.experimental.pallas import tpu as pltpu
from jax.sharding import PartitionSpec as P

BF16 = jnp.bfloat16
F32 = jnp.float32


def pack_kernel(ids_ref, tokens_ref, first_ref, rest_ref, slots_ref):
    experts, tok_rows = slots_ref.shape
    lo = first_ref.shape[1]
    width = tokens_ref.shape[1]
    expert = lax.broadcasted_iota(jnp.int32, (experts, tok_rows), 0)
    chosen = expert == ids_ref[0:1, :]
    for k in range(1, ids_ref.shape[0]):
        chosen = jnp.logical_or(chosen, expert == ids_ref[k : k + 1, :])
    before = lax.broadcasted_iota(jnp.int32, (tok_rows, tok_rows), 0)
    after = lax.broadcasted_iota(jnp.int32, (tok_rows, tok_rows), 1)
    earlier = jnp.where(before < after, 1.0, 0.0).astype(BF16)
    ranks = jnp.dot(jnp.where(chosen, 1.0, 0.0).astype(BF16), earlier, preferred_element_type=F32)
    slots = jnp.where(chosen, ranks, -1.0)
    slots_ref[...] = slots
    slot = lax.broadcasted_iota(jnp.int32, (experts, lo, tok_rows), 1).astype(F32)
    spread = jnp.broadcast_to(slots[:, None, :], (experts, lo, tok_rows))
    for group, packed_ref in enumerate((first_ref, rest_ref)):
        picks = jnp.where(spread == slot + lo * group, 1.0, 0.0).reshape(experts * lo, tok_rows).astype(BF16)
        values = jnp.dot(picks, tokens_ref[...], preferred_element_type=F32)
        packed_ref[...] = values.reshape(experts, lo, width).astype(BF16)


def pack_rows(ids, tokens, experts, lo):
    tok_rows, width = tokens.shape
    packed = jax.ShapeDtypeStruct((experts, lo, width), BF16)
    return pl.pallas_call(
        pack_kernel,
        out_shape=(packed, packed, jax.ShapeDtypeStruct((experts, tok_rows), F32)),
        in_specs=[pl.BlockSpec(memory_space=pltpu.VMEM)] * 2,
        out_specs=[pl.BlockSpec(memory_space=pltpu.VMEM)] * 3,
        name="pack_rows",
    )(ids, tokens)


def on_device(tokens, expert_ids, gate_weights, gate_proj, up_proj, down_proj):
    n_hidden = lax.axis_size("hidden")
    here = lax.axis_index("hidden")
    experts_all = gate_proj.shape[0] * lax.axis_size("expert")
    tok_rows, width = tokens.shape
    units = gate_proj.shape[1]
    top_count = expert_ids.shape[1]
    capacity = 2 * tok_rows * top_count // experts_all
    lo = capacity // 2
    rows = experts_all * lo

    def exchange(values):
        return lax.all_to_all(values, "expert", split_axis=0, concat_axis=0, tiled=True)

    def fetch(values, ahead):
        return lax.ppermute(values, "hidden", [(i, (i - ahead) % n_hidden) for i in range(n_hidden)])

    def around(values, group):
        ahead = behind = values
        yield 0, values
        for step in range(1, n_hidden // 2):
            behind, ahead = fetch(behind, -1), fetch(ahead, 1)
            yield n_hidden - step, behind
            yield step, ahead
        half = values.shape[0] // 2
        if group == 0:
            yield n_hidden // 2, fetch(behind, -1)
        else:
            yield n_hidden // 2, jnp.concatenate([fetch(behind[:half], -1), fetch(ahead[half:], 1)], axis=0)

    first, rest, slots = pack_rows(expert_ids.T, tokens, experts_all, lo)

    both = jnp.concatenate([gate_proj[0], up_proj[0]], axis=0)
    both = lax.dynamic_slice_in_dim(jnp.concatenate([both, both], axis=1), here * width, n_hidden * width, axis=1)
    down = lax.dynamic_slice_in_dim(
        jnp.concatenate([down_proj[0], down_proj[0]], axis=0), here * units, n_hidden * units, axis=0
    )
    arrived = exchange(first)
    arrived, rest, both, down = lax.optimization_barrier((arrived, rest, both, down))
    arrived = [arrived, exchange(rest)]

    activation = []
    for group in range(2):
        total = 0.0
        for ahead, block in around(arrived[group].reshape(rows, width), group):
            weight = both[:, ahead * width : (ahead + 1) * width]
            total = total + jnp.einsum("fd,rd->fr", weight, block, preferred_element_type=F32)
        activation.append((jax.nn.silu(total[:units]) * total[units:]).astype(BF16))
    activation = jnp.concatenate(activation, axis=1)

    picks = slots[:, None, :] == jnp.arange(capacity, dtype=F32)[None, :, None]
    hits = expert_ids[:, :, None] == jnp.arange(experts_all, dtype=jnp.int32)
    weights = jnp.sum(jnp.where(hits, gate_weights[:, :, None], 0.0), axis=1)
    combine = jnp.where(picks, weights.T[:, None, :], 0.0)
    combine, activation = lax.optimization_barrier((combine, activation))

    def out_sums(block, ahead):
        return jnp.einsum("fr,fd->rd", block, down[ahead * units : (ahead + 1) * units], preferred_element_type=F32)

    across = n_hidden // 2
    total = out_sums(activation, 0)
    ahead = behind = activation
    for step in range(1, across):
        behind, ahead = fetch(behind, -1), fetch(ahead, 1)
        total = total + out_sums(behind, n_hidden - step) + out_sums(ahead, step)
    opposite = jnp.concatenate([fetch(behind[:, :rows], -1), fetch(ahead[:, rows:], 1)], axis=1)
    total = (total + out_sums(opposite, across)).astype(BF16)
    total = total.reshape(2, experts_all, lo, width).transpose(1, 0, 2, 3).reshape(experts_all, capacity, width)
    returned = exchange(total)
    mixed = jnp.einsum(
        "est,esd->td",
        combine,
        returned.astype(F32),
        precision=lax.Precision.HIGHEST,
        preferred_element_type=F32,
    )
    return mixed.astype(BF16)


def solution(mesh):
    in_specs = (
        P("expert", "hidden"),
        P("expert", None),
        P("expert", None),
        P("expert", "hidden", None),
        P("expert", "hidden", None),
        P("expert", None, "hidden"),
    )
    out_specs = P("expert", "hidden")
    return jax.shard_map(
        on_device, mesh=mesh, in_specs=in_specs, out_specs=out_specs, check_vma=False
    )
```

```python
import jax
import jax.numpy as jnp
from jax import lax
from jax.experimental import pallas as pl
from jax.experimental.pallas import tpu as pltpu
from jax.sharding import PartitionSpec as P

BF16 = jnp.bfloat16
F32 = jnp.float32


def pack_kernel(ids_ref, tokens_ref, packed_ref, slots_ref):
    experts, tok_rows = slots_ref.shape
    capacity, width = packed_ref.shape[1:]
    expert = lax.broadcasted_iota(jnp.int32, (experts, tok_rows), 0)
    chosen = expert == ids_ref[0:1, :]
    for k in range(1, ids_ref.shape[0]):
        chosen = jnp.logical_or(chosen, expert == ids_ref[k : k + 1, :])
    before = lax.broadcasted_iota(jnp.int32, (tok_rows, tok_rows), 0)
    after = lax.broadcasted_iota(jnp.int32, (tok_rows, tok_rows), 1)
    earlier = jnp.where(before < after, 1.0, 0.0).astype(BF16)
    ranks = jnp.dot(jnp.where(chosen, 1.0, 0.0).astype(BF16), earlier, preferred_element_type=F32)
    slots = jnp.where(chosen, ranks, -1.0)
    slots_ref[...] = slots
    slot = lax.broadcasted_iota(jnp.int32, (experts, capacity, tok_rows), 1).astype(F32)
    spread = jnp.broadcast_to(slots[:, None, :], (experts, capacity, tok_rows))
    picks = jnp.where(spread == slot, 1.0, 0.0).reshape(experts * capacity, tok_rows).astype(BF16)
    values = jnp.dot(picks, tokens_ref[...], preferred_element_type=F32)
    packed_ref[...] = values.reshape(experts, capacity, width).astype(BF16)


def pack_rows(ids, tokens, experts, capacity):
    tok_rows, width = tokens.shape
    return pl.pallas_call(
        pack_kernel,
        out_shape=(
            jax.ShapeDtypeStruct((experts, capacity, width), BF16),
            jax.ShapeDtypeStruct((experts, tok_rows), F32),
        ),
        in_specs=[pl.BlockSpec(memory_space=pltpu.VMEM)] * 2,
        out_specs=[pl.BlockSpec(memory_space=pltpu.VMEM)] * 2,
        name="pack_rows",
    )(ids, tokens)


def on_device(tokens, expert_ids, gate_weights, gate_proj, up_proj, down_proj):
    n_hidden = lax.axis_size("hidden")
    here = lax.axis_index("hidden")
    experts_all = gate_proj.shape[0] * lax.axis_size("expert")
    tok_rows, width = tokens.shape
    units = gate_proj.shape[1]
    top_count = expert_ids.shape[1]
    capacity = 2 * tok_rows * top_count // experts_all
    rows = experts_all * capacity // 2

    def exchange(values):
        return lax.all_to_all(values, "expert", split_axis=0, concat_axis=0, tiled=True)

    def fetch(values, ahead):
        return lax.ppermute(values, "hidden", [(i, (i - ahead) % n_hidden) for i in range(n_hidden)])

    def around(values, group):
        ahead = behind = values
        yield 0, values
        for step in range(1, n_hidden // 2):
            behind, ahead = fetch(behind, -1), fetch(ahead, 1)
            yield n_hidden - step, behind
            yield step, ahead
        yield n_hidden // 2, fetch(behind, -1) if group == 0 else fetch(ahead, 1)

    packed, slots = pack_rows(expert_ids.T, tokens, experts_all, capacity)

    both = jnp.concatenate([gate_proj[0], up_proj[0]], axis=0)
    both = lax.dynamic_slice_in_dim(jnp.concatenate([both, both], axis=1), here * width, n_hidden * width, axis=1)
    down = lax.dynamic_slice_in_dim(
        jnp.concatenate([down_proj[0], down_proj[0]], axis=0), here * units, n_hidden * units, axis=0
    )
    arrived = exchange(packed).reshape(2 * rows, width)
    arrived, both, down = lax.optimization_barrier((arrived, both, down))

    activation = []
    for group in range(2):
        total = 0.0
        for ahead, block in around(arrived[group * rows : (group + 1) * rows], group):
            weight = both[:, ahead * width : (ahead + 1) * width]
            total = total + jnp.einsum("fd,rd->fr", weight, block, preferred_element_type=F32)
        activation.append((jax.nn.silu(total[:units]) * total[units:]).astype(BF16))
    activation = jnp.concatenate(activation, axis=1)

    picks = slots[:, None, :] == jnp.arange(capacity, dtype=F32)[None, :, None]
    hits = expert_ids[:, :, None] == jnp.arange(experts_all, dtype=jnp.int32)
    weights = jnp.sum(jnp.where(hits, gate_weights[:, :, None], 0.0), axis=1)
    combine = jnp.where(picks, weights.T[:, None, :], 0.0)
    combine, activation = lax.optimization_barrier((combine, activation))

    def out_sums(block, ahead):
        return jnp.einsum("fr,fd->rd", block, down[ahead * units : (ahead + 1) * units], preferred_element_type=F32)

    across = n_hidden // 2
    total = out_sums(activation, 0)
    ahead = behind = activation
    for step in range(1, across):
        behind, ahead = fetch(behind, -1), fetch(ahead, 1)
        total = total + out_sums(behind, n_hidden - step) + out_sums(ahead, step)
    opposite = jnp.concatenate([fetch(behind[:, :rows], -1), fetch(ahead[:, rows:], 1)], axis=1)
    total = (total + out_sums(opposite, across)).astype(BF16)
    returned = exchange(total.reshape(experts_all, capacity, width))
    mixed = jnp.einsum(
        "est,esd->td",
        combine,
        returned.astype(F32),
        precision=lax.Precision.HIGHEST,
        preferred_element_type=F32,
    )
    return mixed.astype(BF16)


def solution(mesh):
    in_specs = (
        P("expert", "hidden"),
        P("expert", None),
        P("expert", None),
        P("expert", "hidden", None),
        P("expert", "hidden", None),
        P("expert", None, "hidden"),
    )
    out_specs = P("expert", "hidden")
    return jax.shard_map(
        on_device, mesh=mesh, in_specs=in_specs, out_specs=out_specs, check_vma=False
    )
```
